512 devices in a mesh: expert: 4 (over z_hi, core), rep: 4 (over y), hid: 32 (over x, z_lo).
Axes of the slice: x: 4, y: 4, z: 16 (z_hi: 2, z_lo: 8; z = z_hi * 8 + z_lo), core: 2. Of those that a mesh axis runs over, the one named last changes fastest.
Arguments:
- tokens: bfloat16 [1024, 6144], P(('expert', 'hid'), 'rep'), may hold values from -6 to 6
- norm_gain: float32 [6144], P('rep'), may hold values from 0.25 to 1.75
- expert_ids: int32 [1024, 2], P(('expert', 'hid')), may hold values from 0 to 3, as said below
- slot_ids: int32 [1024, 2], P(('expert', 'hid')), may hold values from 0 to 4, as said below
- w_gate: bfloat16 [4, 6144, 8192], P('expert', 'rep', 'hid'), may hold values from -0.078125 to 0.078125
- w_up: bfloat16 [4, 6144, 8192], P('expert', 'rep', 'hid'), may hold values from -0.078125 to 0.078125
- grad_gate: bfloat16 [4, 640, 8192], P('expert', None, 'hid'), may hold values from -1.1953125 to 1.1953125
- grad_up: bfloat16 [4, 640, 8192], P('expert', None, 'hid'), may hold values from -1.1953125 to 1.1953125
Outputs:
- grad_w_gate: bfloat16 [4, 6144, 8192], P('expert', 'rep', 'hid')
- grad_w_up: bfloat16 [4, 6144, 8192], P('expert', 'rep', 'hid')
- grad_tokens: bfloat16 [1024, 6144], P(('expert', 'hid'), 'rep')
The draws below stay inside these ranges and needn't reach their ends.
Inputs may be any that keep to these rules, and one draw needn't show every extreme that they name: `expert_ids`: each token names two different experts; among the 8 tokens of one block, no expert is named more than 5 times and some expert exactly 5 times. Within one block of 8 tokens, the pairs (expert_ids[t, k], slot_ids[t, k]) are all different.
All inputs are finite; a program needn't handle non-finite values.
Results may differ from the reference program's by a relative error of at most 0.0049.
Values may be sent and summed in bfloat16 or wider, within the bound.
No kernel may reach another device: no remote copies, remote signals or barrier semaphores. Data moves between devices by JAX's collectives and lax.ppermute only.
A program may use at most 64 MiB of HBM per device.

```python
import jax
import jax.numpy as jnp
from jax import lax

D = 6144
FF = 8192
TOK_DEV = 8
EXPERTS = 4
HSPLIT = 32
CAP = 5
ROWS = 640
TOKENS = 1024


def routing_plan(key):
    blocks = TOKENS // TOK_DEV
    slots_all = EXPERTS * CAP
    dropped = slots_all - 2 * TOK_DEV
    block_keys = jax.random.split(jax.random.fold_in(key, 101), blocks)

    def one_block(block_key):
        key_full, key_score, key_order, key_flip = jax.random.split(block_key, 4)
        full_expert = jax.random.randint(key_full, (), 0, EXPERTS)
        position = jnp.arange(slots_all, dtype=jnp.int32)
        scores = jax.random.permutation(key_score, slots_all).astype(jnp.int32)
        scores = jnp.where(position // CAP == full_expert, slots_all + position, scores)
        ranked = jnp.argsort(scores)
        kept = jnp.sort(ranked[dropped:]).astype(jnp.int32)
        order = jax.random.permutation(key_order, TOK_DEV)
        first = kept[:TOK_DEV][order]
        second = kept[TOK_DEV:][order]
        flipped = jax.random.randint(key_flip, (TOK_DEV,), 0, 2) == 1
        leading = jnp.where(flipped, second, first)
        trailing = jnp.where(flipped, first, second)
        return jnp.stack([leading, trailing], axis=1)
    return jax.vmap(one_block)(block_keys).reshape(TOKENS, 2).astype(jnp.int32)


def draw_expert_ids(key, part):
    return routing_plan(key) // CAP


def draw_slot_ids(key, part):
    return routing_plan(key) % CAP


def with_spikes(array, rng, source, target, parts, factor):
    def block_of(axis_at):
        return (jnp.arange(array.shape[axis_at]) // (array.shape[axis_at] // parts)).reshape((-1,) + (1,) * (array.ndim - 1 - axis_at))

    one_side = jax.random.permutation(rng, parts)[block_of(target)]
    other_side = (block_of(target) + parts // 2) % parts
    return jnp.where((block_of(source) == one_side) | (block_of(source) == other_side), factor * array, array)


def steps_of(rng, shape, cuts, least, largest):
    def one(axis_at, blocks):
        steps = jax.random.uniform(jax.random.fold_in(jax.random.fold_in(rng, 6), axis_at), (blocks,), jnp.float32, least / len(cuts), largest / len(cuts))
        return jnp.repeat(jnp.exp(steps), shape[axis_at] // blocks).reshape((-1,) + (1,) * (len(shape) - axis_at - 1))

    loudness = one(*cuts[0])
    for cut in cuts[1:]:
        loudness = loudness * one(*cut)
    return loudness


def noise(rng, shape, width, most, cuts=(), kind=jnp.bfloat16):
    entries = width * jax.random.normal(rng, shape, jnp.float32)
    if cuts:
        entries = entries * steps_of(rng, shape, cuts, -0.22, 0.18)
    return jnp.clip(entries, -most, most).astype(kind)


def bell_draw_with(key, dims, width, limit, shards, heavy, kind=jnp.bfloat16):
    result = width * jax.random.normal(key, dims, jnp.float32)
    if shards:
        result = result * steps_of(key, dims, shards, -0.22, 0.18)
    return jnp.clip(with_spikes(result, jax.random.fold_in(key, 3), *heavy), -limit, limit).astype(kind)


def setup_inputs(seed: int = 0) -> dict:
    key_of = jax.random.split(jax.random.key(seed), 9)
    return {
        "tokens": noise(key_of[0], (TOKENS, D), 1.0, 6.0, ((0, 128), (1, 4))),
        "norm_gain": jnp.clip(1.0 + 0.15 * jax.random.normal(key_of[1], (D,), jnp.float32), 0.25, 1.75),
        "expert_ids": draw_expert_ids(jax.random.fold_in(key_of[8], 71), 0),
        "slot_ids": draw_slot_ids(jax.random.fold_in(key_of[8], 71), 0),
        "w_gate": noise(key_of[4], (EXPERTS, D, FF), D ** -0.5, 0.078125, ((0, 4), (1, 4), (2, 32))),
        "w_up": noise(key_of[5], (EXPERTS, D, FF), D ** -0.5, 0.078125, ((0, 4), (1, 4), (2, 32))),
        "grad_gate": bell_draw_with(key_of[6], (EXPERTS, ROWS, FF), 0.15, 1.1953125, ((0, 4), (2, 32)), (2, 1, 32, 2.75)),
        "grad_up": noise(key_of[7], (EXPERTS, ROWS, FF), 0.15, 1.1953125, ((0, 4), (2, 32))),
    }


def reference(tokens, norm_gain, expert_ids, slot_ids, w_gate, w_up, grad_gate, grad_up):
    values = tokens.astype(jnp.float32)
    inverse_rms = lax.rsqrt(lax.optimization_barrier(jnp.mean(values * values, axis=1, keepdims=True)) + 1e-05)
    scaled_in = values * inverse_rms
    normed = (scaled_in * norm_gain).astype(jnp.bfloat16)
    block_index = jnp.arange(TOKENS, dtype=jnp.int32) // TOK_DEV
    source_group = block_index // HSPLIT
    source_hid = block_index % HSPLIT
    row_base = (source_hid * EXPERTS + source_group) * CAP
    row_index = (row_base[:, None] + slot_ids).astype(jnp.int32)
    expert_rows = jnp.zeros((EXPERTS, ROWS, D), normed.dtype)
    for member in range(2):
        expert_rows = expert_rows.at[expert_ids[:, member], row_index[:, member]].set(normed)
    gate_list = []
    up_list = []
    row_list = []
    for expert in range(EXPERTS):
        gate_list.append(jnp.dot(expert_rows[expert].T, grad_gate[expert], preferred_element_type=jnp.float32).astype(jnp.bfloat16))
        up_list.append(jnp.dot(expert_rows[expert].T, grad_up[expert], preferred_element_type=jnp.float32).astype(jnp.bfloat16))
        summed = jnp.dot(grad_gate[expert], w_gate[expert].T, preferred_element_type=jnp.float32)
        summed = summed + jnp.dot(grad_up[expert], w_up[expert].T, preferred_element_type=jnp.float32)
        row_list.append(summed.astype(jnp.bfloat16))
    grad_w_gate = jnp.stack(gate_list)
    grad_w_up = jnp.stack(up_list)
    row_grads = jnp.stack(row_list)
    normed_grad = jnp.zeros((TOKENS, D), jnp.float32)
    for member in range(2):
        normed_grad = normed_grad + row_grads[expert_ids[:, member], row_index[:, member]].astype(jnp.float32)
    scaled = normed_grad * norm_gain
    dotted = lax.optimization_barrier(jnp.mean(scaled * scaled_in, axis=1, keepdims=True))
    grad_tokens = (inverse_rms * (scaled - scaled_in * dotted)).astype(jnp.bfloat16)
    return (grad_w_gate, grad_w_up, grad_tokens)
```

```python
import jax
import jax.numpy as jnp
from jax import lax
from jax.sharding import Mesh
from jax.sharding import PartitionSpec as P

D = 6144
CAP = 5
TOK = 8
RING = ("zh", "zl")
LANES = 128


def exchange(x, axis):
    return lax.all_to_all(x, axis, 0, 0, tiled=True)


def copy_for_each(x, axis):
    size = lax.axis_size(axis)
    return exchange(jnp.broadcast_to(x[None], (size, *x.shape)), axis)


def feature_total(partial_value):
    return copy_for_each(partial_value[None], "rep").sum(axis=(0, 1))


def swap_cores(x):
    return lax.ppermute(x, "core", [(0, 1), (1, 0)])


def on_device(tokens, norm_gain, expert_ids, slot_ids, w_gate, w_up, grad_gate, grad_up):
    zh_n, core_n, x_n, zl_n = (lax.axis_size(a) for a in ("zh", "core", "x", "zl"))
    ring_n = zh_n * zl_n
    line_tokens = ring_n * TOK
    line_rows = zl_n * zh_n * core_n * CAP
    width = tokens.shape[1]
    core = lax.axis_index("core")
    mine = lax.axis_index("zh") * core_n + core
    partner = lax.axis_index("zh") * core_n + (1 - core)

    unit_contract = (((1,), (1,)), ((), ()))
    part = lax.dot_general(
        grad_gate[0], w_gate[0], unit_contract, preferred_element_type=jnp.float32
    ) + lax.dot_general(grad_up[0], w_up[0], unit_contract, preferred_element_type=jnp.float32)
    part = part.astype(jnp.bfloat16).reshape(x_n, line_rows, width)

    values = tokens.astype(jnp.float32)
    square_sums = feature_total(jnp.sum(values * values, axis=1))
    inverse_rms = lax.rsqrt(square_sums / D + 1e-05)[:, None]
    scaled_in = values * inverse_rms
    normed = (scaled_in * norm_gain).astype(jnp.bfloat16)
    code = (expert_ids * CAP + slot_ids).astype(jnp.bfloat16)
    tagged = jnp.concatenate([normed, jnp.pad(code, ((0, 0), (0, LANES - 2)))], axis=1)

    line = copy_for_each(tagged, RING).reshape(line_tokens, width + LANES)
    line_normed = line[:, :width]
    codes = line[:, width : width + 2].astype(jnp.int32)
    token = jnp.arange(line_tokens, dtype=jnp.int32)
    block = token // TOK
    base = (((block % zl_n) * zh_n + block // zl_n) * core_n + core) * CAP

    def rows_of(expert):
        slot = codes - expert * CAP
        return jnp.where((slot >= 0) & (slot < CAP), base[:, None] + slot, -1)

    row = jnp.arange(line_rows, dtype=jnp.int32)

    def choice(expert):
        at = rows_of(expert)
        return ((at[:, 0][:, None] == row[None]) | (at[:, 1][:, None] == row[None])).astype(
            jnp.bfloat16
        )

    to_mine = choice(mine)
    to_partner = choice(partner)
    first = (((0,), (0,)), ((), ()))

    def rows_from(chosen):
        return lax.dot_general(
            chosen, line_normed, first, preferred_element_type=jnp.float32
        ).astype(jnp.bfloat16)

    own_rows = rows_from(to_mine) + swap_cores(rows_from(to_partner))
    gathered = copy_for_each(own_rows, "x").reshape(x_n * line_rows, width)
    new_gate = lax.dot_general(gathered, grad_gate[0], first, preferred_element_type=jnp.float32)
    new_up = lax.dot_general(gathered, grad_up[0], first, preferred_element_type=jnp.float32)

    line_sum = exchange(part, "x").astype(jnp.float32).sum(axis=0).astype(jnp.bfloat16)
    other_sum = swap_cores(line_sum)
    by_token = jnp.dot(to_mine, line_sum, preferred_element_type=jnp.float32) + jnp.dot(
        to_partner, other_sum, preferred_element_type=jnp.float32
    )
    by_token = by_token.astype(jnp.bfloat16).reshape(ring_n, TOK, width)
    normed_grad = exchange(by_token, RING).astype(jnp.float32).sum(axis=0)

    scaled = normed_grad * norm_gain
    dotted = feature_total(jnp.sum(scaled * scaled_in, axis=1)) / D
    grad_tokens = (inverse_rms * (scaled - scaled_in * dotted[:, None])).astype(jnp.bfloat16)
    return (new_gate.astype(jnp.bfloat16)[None], new_up.astype(jnp.bfloat16)[None], grad_tokens)


def solution(mesh):
    physical = Mesh(mesh.devices.reshape(2, 2, 4, 4, 8), ("zh", "core", "rep", "x", "zl"))
    expert, hid = ("zh", "core"), ("x", "zl")
    placed = (
        P(expert + hid, "rep"),
        P("rep"),
        P(expert + hid, None),
        P(expert + hid, None),
        P(expert, "rep", hid),
        P(expert, "rep", hid),
        P(expert, None, hid),
        P(expert, None, hid),
    )
    return jax.shard_map(
        on_device,
        mesh=physical,
        in_specs=placed,
        out_specs=(P(expert, "rep", hid), P(expert, "rep", hid), P(expert + hid, "rep")),
        check_vma=False,
    )
```

```python
import jax
import jax.numpy as jnp
from jax import lax
from jax.sharding import Mesh
from jax.sharding import PartitionSpec as P

D = 6144
CAP = 5
TOK = 8
RING = ("zh", "zl")
LANES = 128


def exchange(x, axis):
    return lax.all_to_all(x, axis, 0, 0, tiled=True)


def copy_for_each(x, axis):
    size = lax.axis_size(axis)
    return exchange(jnp.broadcast_to(x[None], (size, *x.shape)), axis)


def feature_total(partial_value):
    return copy_for_each(partial_value[None], "rep").sum(axis=(0, 1))


def along_x(x, step):
    size = lax.axis_size("x")
    return lax.ppermute(x, "x", [(i, (i + step) % size) for i in range(size)])


def swap_cores(x):
    return lax.ppermute(x, "core", [(0, 1), (1, 0)])


def on_device(tokens, norm_gain, expert_ids, slot_ids, w_gate, w_up, grad_gate, grad_up):
    zh_n, core_n, x_n, zl_n = (lax.axis_size(a) for a in ("zh", "core", "x", "zl"))
    ring_n = zh_n * zl_n
    line_tokens = ring_n * TOK
    line_rows = zl_n * zh_n * core_n * CAP
    width = tokens.shape[1]
    core = lax.axis_index("core")
    mine = lax.axis_index("zh") * core_n + core
    partner = lax.axis_index("zh") * core_n + (1 - core)

    unit_contract = (((1,), (1,)), ((), ()))
    here = lax.axis_index("x")

    def part_for(step):
        at = lax.rem(here + step, x_n) * line_rows
        gate = lax.dynamic_slice_in_dim(grad_gate[0], at, line_rows)
        up = lax.dynamic_slice_in_dim(grad_up[0], at, line_rows)
        return lax.dot_general(
            gate, w_gate[0], unit_contract, preferred_element_type=jnp.float32
        ) + lax.dot_general(up, w_up[0], unit_contract, preferred_element_type=jnp.float32)

    arriving = [
        along_x(part_for(step).astype(jnp.bfloat16), step).astype(jnp.float32)
        for step in (2, 1, 3)
    ]
    kept = part_for(0)

    values = tokens.astype(jnp.float32)
    square_sums = feature_total(jnp.sum(values * values, axis=1))
    inverse_rms = lax.rsqrt(square_sums / D + 1e-05)[:, None]
    scaled_in = values * inverse_rms
    normed = (scaled_in * norm_gain).astype(jnp.bfloat16)
    code = (expert_ids * CAP + slot_ids).astype(jnp.bfloat16)
    tagged = jnp.concatenate([normed, jnp.pad(code, ((0, 0), (0, LANES - 2)))], axis=1)

    line = copy_for_each(tagged, RING).reshape(line_tokens, width + LANES)
    line_normed = line[:, :width]
    codes = line[:, width : width + 2].astype(jnp.int32)
    token = jnp.arange(line_tokens, dtype=jnp.int32)
    block = token // TOK
    base = (((block % zl_n) * zh_n + block // zl_n) * core_n + core) * CAP

    def rows_of(expert):
        slot = codes - expert * CAP
        return jnp.where((slot >= 0) & (slot < CAP), base[:, None] + slot, -1)

    row = jnp.arange(line_rows, dtype=jnp.int32)

    def choice(expert):
        at = rows_of(expert)
        return ((at[:, 0][:, None] == row[None]) | (at[:, 1][:, None] == row[None])).astype(
            jnp.bfloat16
        )

    to_mine = choice(mine)
    to_partner = choice(partner)
    first = (((0,), (0,)), ((), ()))

    def rows_from(chosen):
        return lax.dot_general(
            chosen, line_normed, first, preferred_element_type=jnp.float32
        ).astype(jnp.bfloat16)

    own_rows = rows_from(to_mine) + swap_cores(rows_from(to_partner))
    steps = (0, 1, 3, 2)
    gathered = jnp.concatenate([own_rows] + [along_x(own_rows, step) for step in steps[1:]])

    def in_order(cotangent):
        return jnp.concatenate(
            [
                lax.dynamic_slice_in_dim(
                    cotangent, lax.rem(here - step + x_n, x_n) * line_rows, line_rows
                )
                for step in steps
            ]
        )

    new_gate = lax.dot_general(
        gathered, in_order(grad_gate[0]), first, preferred_element_type=jnp.float32
    )
    new_up = lax.dot_general(
        gathered, in_order(grad_up[0]), first, preferred_element_type=jnp.float32
    )

    line_sum = (kept + arriving[0] + arriving[1] + arriving[2]).astype(jnp.bfloat16)
    other_sum = swap_cores(line_sum)
    by_token = jnp.dot(to_mine, line_sum, preferred_element_type=jnp.float32) + jnp.dot(
        to_partner, other_sum, preferred_element_type=jnp.float32
    )
    by_token = by_token.astype(jnp.bfloat16).reshape(ring_n, TOK, width)
    normed_grad = exchange(by_token, RING).astype(jnp.float32).sum(axis=0)

    scaled = normed_grad * norm_gain
    dotted = feature_total(jnp.sum(scaled * scaled_in, axis=1)) / D
    grad_tokens = (inverse_rms * (scaled - scaled_in * dotted[:, None])).astype(jnp.bfloat16)
    return (new_gate.astype(jnp.bfloat16)[None], new_up.astype(jnp.bfloat16)[None], grad_tokens)


def solution(mesh):
    physical = Mesh(mesh.devices.reshape(2, 2, 4, 4, 8), ("zh", "core", "rep", "x", "zl"))
    expert, hid = ("zh", "core"), ("x", "zl")
    placed = (
        P(expert + hid, "rep"),
        P("rep"),
        P(expert + hid, None),
        P(expert + hid, None),
        P(expert, "rep", hid),
        P(expert, "rep", hid),
        P(expert, None, hid),
        P(expert, None, hid),
    )
    return jax.shard_map(
        on_device,
        mesh=physical,
        in_specs=placed,
        out_specs=(P(expert, "rep", hid), P(expert, "rep", hid), P(expert + hid, "rep")),
        check_vma=False,
    )
```

```python
import jax
import jax.numpy as jnp
from jax import lax
from jax.sharding import Mesh
from jax.sharding import PartitionSpec as P

D = 6144
CAP = 5
TOK = 8
RING = ("zh", "zl")
LANES = 128


def exchange(x, axis):
    return lax.all_to_all(x, axis, 0, 0, tiled=True)


def copy_for_each(x, axis):
    size = lax.axis_size(axis)
    return exchange(jnp.broadcast_to(x[None], (size, *x.shape)), axis)


def feature_total(partial_value):
    return copy_for_each(partial_value[None], "rep").sum(axis=(0, 1))


def along_x(x, step):
    size = lax.axis_size("x")
    return lax.ppermute(x, "x", [(i, (i + step) % size) for i in range(size)])


def swap_cores(x):
    return lax.ppermute(x, "core", [(0, 1), (1, 0)])


def on_device(tokens, norm_gain, expert_ids, slot_ids, w_gate, w_up, grad_gate, grad_up):
    zh_n, core_n, x_n, zl_n = (lax.axis_size(a) for a in ("zh", "core", "x", "zl"))
    ring_n = zh_n * zl_n
    line_tokens = ring_n * TOK
    line_rows = zl_n * zh_n * core_n * CAP
    width = tokens.shape[1]
    core = lax.axis_index("core")
    mine = lax.axis_index("zh") * core_n + core
    partner = lax.axis_index("zh") * core_n + (1 - core)

    unit_contract = (((1,), (1,)), ((), ()))
    here = lax.axis_index("x")

    def part_for(step):
        at = lax.rem(here + step, x_n) * line_rows
        gate = lax.dynamic_slice_in_dim(grad_gate[0], at, line_rows)
        up = lax.dynamic_slice_in_dim(grad_up[0], at, line_rows)
        return lax.dot_general(
            gate, w_gate[0], unit_contract, preferred_element_type=jnp.float32
        ) + lax.dot_general(up, w_up[0], unit_contract, preferred_element_type=jnp.float32)

    arriving = [
        along_x(part_for(step).astype(jnp.bfloat16), step).astype(jnp.float32)
        for step in (2, 1, 3)
    ]
    kept = part_for(0)

    code = (expert_ids * CAP + slot_ids).astype(jnp.bfloat16)
    tagged = jnp.concatenate([tokens, jnp.pad(code, ((0, 0), (0, LANES - 2)))], axis=1)
    line = copy_for_each(tagged, RING).reshape(line_tokens, width + LANES)
    line_values = line[:, :width].astype(jnp.float32)
    codes = line[:, width : width + 2].astype(jnp.int32)

    square_sums = feature_total(jnp.sum(line_values * line_values, axis=1))
    line_rms = lax.rsqrt(square_sums / D + 1e-05)[:, None]
    line_normed = (line_values * line_rms * norm_gain).astype(jnp.bfloat16)
    at_ring = (lax.axis_index("zh") * zl_n + lax.axis_index("zl")) * TOK
    inverse_rms = lax.dynamic_slice_in_dim(line_rms, at_ring, TOK)
    scaled_in = tokens.astype(jnp.float32) * inverse_rms

    token = jnp.arange(line_tokens, dtype=jnp.int32)
    block = token // TOK
    base = (((block % zl_n) * zh_n + block // zl_n) * core_n + core) * CAP

    def rows_of(expert):
        slot = codes - expert * CAP
        return jnp.where((slot >= 0) & (slot < CAP), base[:, None] + slot, -1)

    row = jnp.arange(line_rows, dtype=jnp.int32)

    def choice(expert):
        at = rows_of(expert)
        return ((at[:, 0][:, None] == row[None]) | (at[:, 1][:, None] == row[None])).astype(
            jnp.bfloat16
        )

    to_mine = choice(mine)
    to_partner = choice(partner)
    first = (((0,), (0,)), ((), ()))

    def rows_from(chosen):
        return lax.dot_general(
            chosen, line_normed, first, preferred_element_type=jnp.float32
        ).astype(jnp.bfloat16)

    own_rows = rows_from(to_mine) + swap_cores(rows_from(to_partner))
    steps = (0, 1, 3, 2)
    gathered = jnp.concatenate([own_rows] + [along_x(own_rows, step) for step in steps[1:]])

    def in_order(cotangent):
        return jnp.concatenate(
            [
                lax.dynamic_slice_in_dim(
                    cotangent, lax.rem(here - step + x_n, x_n) * line_rows, line_rows
                )
                for step in steps
            ]
        )

    new_gate = lax.dot_general(
        gathered, in_order(grad_gate[0]), first, preferred_element_type=jnp.float32
    )
    new_up = lax.dot_general(
        gathered, in_order(grad_up[0]), first, preferred_element_type=jnp.float32
    )

    line_sum = (kept + arriving[0] + arriving[1] + arriving[2]).astype(jnp.bfloat16)
    other_sum = swap_cores(line_sum)
    by_token = jnp.dot(to_mine, line_sum, preferred_element_type=jnp.float32) + jnp.dot(
        to_partner, other_sum, preferred_element_type=jnp.float32
    )
    by_token = by_token.astype(jnp.bfloat16).reshape(ring_n, TOK, width)
    normed_grad = exchange(by_token, RING).astype(jnp.float32).sum(axis=0)

    scaled = normed_grad * norm_gain
    dotted = feature_total(jnp.sum(scaled * scaled_in, axis=1)) / D
    grad_tokens = (inverse_rms * (scaled - scaled_in * dotted[:, None])).astype(jnp.bfloat16)
    return (new_gate.astype(jnp.bfloat16)[None], new_up.astype(jnp.bfloat16)[None], grad_tokens)


def solution(mesh):
    physical = Mesh(mesh.devices.reshape(2, 2, 4, 4, 8), ("zh", "core", "rep", "x", "zl"))
    expert, hid = ("zh", "core"), ("x", "zl")
    placed = (
        P(expert + hid, "rep"),
        P("rep"),
        P(expert + hid, None),
        P(expert + hid, None),
        P(expert, "rep", hid),
        P(expert, "rep", hid),
        P(expert, None, hid),
        P(expert, None, hid),
    )
    return jax.shard_map(
        on_device,
        mesh=physical,
        in_specs=placed,
        out_specs=(P(expert, "rep", hid), P(expert, "rep", hid), P(expert + hid, "rep")),
        check_vma=False,
    )
```

```python
import jax
import jax.numpy as jnp
from jax import lax
from jax.sharding import Mesh
from jax.sharding import PartitionSpec as P


D = 6144
CAP = 5
TOK = 8
RING = ("zh", "zl")
LANES = 128


def exchange(x, axis):
    return lax.all_to_all(x, axis, 0, 0, tiled=True)


def copy_for_each(x, axis):
    size = lax.axis_size(axis)
    return exchange(jnp.broadcast_to(x[None], (size, *x.shape)), axis)


def feature_total(partial_value):
    return copy_for_each(partial_value[None], "rep").sum(axis=(0, 1))


def along(x, axis, step):
    size = lax.axis_size(axis)
    return lax.ppermute(x, axis, [(i, (i + step) % size) for i in range(size)])


def swap_cores(x):
    return lax.ppermute(x, "core", [(0, 1), (1, 0)])


def on_device(tokens, norm_gain, expert_ids, slot_ids, w_gate, w_up, grad_gate, grad_up):
    zh_n, core_n, x_n, zl_n = (lax.axis_size(a) for a in ("zh", "core", "x", "zl"))
    ring_n = zh_n * zl_n
    line_tokens = ring_n * TOK
    line_rows = zl_n * zh_n * core_n * CAP
    width = tokens.shape[1]
    core = lax.axis_index("core")
    mine = lax.axis_index("zh") * core_n + core
    partner = lax.axis_index("zh") * core_n + (1 - core)

    unit_contract = (((1,), (1,)), ((), ()))
    here = lax.axis_index("x")

    def part_for(step):
        at = lax.rem(here + step, x_n) * line_rows
        gate = lax.dynamic_slice_in_dim(grad_gate[0], at, line_rows)
        up = lax.dynamic_slice_in_dim(grad_up[0], at, line_rows)
        return lax.dot_general(
            gate, w_gate[0], unit_contract, preferred_element_type=jnp.float32
        ) + lax.dot_general(up, w_up[0], unit_contract, preferred_element_type=jnp.float32)

    arriving = []
    for step in (2, 1, 3):
        piece = part_for(step).astype(jnp.bfloat16)
        arriving.append(along(piece, "x", step).astype(jnp.float32))
    kept = part_for(0)

    code = (expert_ids * CAP + slot_ids).astype(jnp.bfloat16)
    tagged = jnp.concatenate([tokens, jnp.pad(code, ((0, 0), (0, LANES - 2)))], axis=1)
    line = copy_for_each(tagged, RING).reshape(line_tokens, width + LANES)
    line_values = line[:, :width]
    codes = line[:, width : width + 2].astype(jnp.int32)
    token = jnp.arange(line_tokens, dtype=jnp.int32)
    block = token // TOK
    base = (((block % zl_n) * zh_n + block // zl_n) * core_n + core) * CAP

    def rows_of(expert):
        slot = codes - expert * CAP
        return jnp.where((slot >= 0) & (slot < CAP), base[:, None] + slot, -1)

    row = jnp.arange(line_rows, dtype=jnp.int32)

    def choice(expert):
        at = rows_of(expert)
        return ((at[:, 0][:, None] == row[None]) | (at[:, 1][:, None] == row[None])).astype(
            jnp.bfloat16
        )

    to_mine = choice(mine)
    to_partner = choice(partner)
    first = (((0,), (0,)), ((), ()))

    def rows_from(chosen):
        return lax.dot_general(
            chosen, line_values, first, preferred_element_type=jnp.float32
        ).astype(jnp.bfloat16)

    own_rows = rows_from(to_mine) + swap_cores(rows_from(to_partner))
    steps = (0, 1, 3, 2)
    pieces = [own_rows]
    pieces += [along(own_rows, "x", step) for step in steps[1:]]

    values = tokens.astype(jnp.float32)
    squares = [jnp.sum(jnp.square(piece.astype(jnp.float32)), axis=1) for piece in pieces]
    squares += [jnp.sum(values * values, axis=1)]
    count = x_n * line_rows + TOK
    squares = jnp.pad(jnp.concatenate(squares), (0, -count % LANES)).reshape(-1, LANES)
    others = [along(squares, "rep", step) for step in (1, 3, 2)]
    squares = squares + others[0] + others[1] + others[2]
    rms = lax.rsqrt(squares / D + 1e-05).reshape(-1)[:count, None]
    row_rms, inverse_rms = rms[:-TOK], rms[-TOK:]
    scaled_in = values * inverse_rms
    raw = jnp.concatenate(pieces).astype(jnp.float32)
    gathered = (raw * row_rms * norm_gain).astype(jnp.bfloat16)

    def in_order(cotangent):
        return jnp.concatenate(
            [
                lax.dynamic_slice_in_dim(
                    cotangent, lax.rem(here - step + x_n, x_n) * line_rows, line_rows
                )
                for step in steps
            ]
        )

    new_gate = lax.dot_general(
        gathered, in_order(grad_gate[0]), first, preferred_element_type=jnp.float32
    )
    new_up = lax.dot_general(
        gathered, in_order(grad_up[0]), first, preferred_element_type=jnp.float32
    )

    line_sum = (kept + arriving[0] + arriving[1] + arriving[2]).astype(jnp.bfloat16)
    other_sum = swap_cores(line_sum)
    by_token = jnp.dot(to_mine, line_sum, preferred_element_type=jnp.float32) + jnp.dot(
        to_partner, other_sum, preferred_element_type=jnp.float32
    )
    by_token = by_token.astype(jnp.bfloat16).reshape(ring_n, TOK, width)
    normed_grad = exchange(by_token, RING).astype(jnp.float32).sum(axis=0)

    scaled = normed_grad * norm_gain
    dotted = feature_total(jnp.sum(scaled * scaled_in, axis=1)) / D
    grad_tokens = (inverse_rms * (scaled - scaled_in * dotted[:, None])).astype(jnp.bfloat16)
    return (new_gate.astype(jnp.bfloat16)[None], new_up.astype(jnp.bfloat16)[None], grad_tokens)


def solution(mesh):
    physical = Mesh(mesh.devices.reshape(2, 2, 4, 4, 8), ("zh", "core", "rep", "x", "zl"))
    expert, hid = ("zh", "core"), ("x", "zl")
    placed = (
        P(expert + hid, "rep"),
        P("rep"),
        P(expert + hid, None),
        P(expert + hid, None),
        P(expert, "rep", hid),
        P(expert, "rep", hid),
        P(expert, None, hid),
        P(expert, None, hid),
    )

    return jax.shard_map(
        on_device,
        mesh=physical,
        in_specs=placed,
        out_specs=(P(expert, "rep", hid), P(expert, "rep", hid), P(expert + hid, "rep")),
        check_vma=False,
    )
```

```python
import jax
import jax.numpy as jnp
from jax import lax
from jax.sharding import Mesh
from jax.sharding import PartitionSpec as P


D = 6144
CAP = 5
TOK = 8
RING = ("zh", "zl")
LANES = 128


def exchange(x, axis):
    return lax.all_to_all(x, axis, 0, 0, tiled=True)


def copy_for_each(x, axis):
    size = lax.axis_size(axis)
    return exchange(jnp.broadcast_to(x[None], (size, *x.shape)), axis)


def feature_total(partial_value):
    return copy_for_each(partial_value[None], "rep").sum(axis=(0, 1))


def along(x, axis, step):
    size = lax.axis_size(axis)
    return lax.ppermute(x, axis, [(i, (i + step) % size) for i in range(size)])


def swap_cores(x):
    return lax.ppermute(x, "core", [(0, 1), (1, 0)])


def on_device(tokens, norm_gain, expert_ids, slot_ids, w_gate, w_up, grad_gate, grad_up):
    zh_n, core_n, x_n, zl_n = (lax.axis_size(a) for a in ("zh", "core", "x", "zl"))
    ring_n = zh_n * zl_n
    line_tokens = ring_n * TOK
    line_rows = zl_n * zh_n * core_n * CAP
    width = tokens.shape[1]
    core = lax.axis_index("core")
    mine = lax.axis_index("zh") * core_n + core
    partner = lax.axis_index("zh") * core_n + (1 - core)

    unit_contract = (((1,), (1,)), ((), ()))
    here = lax.axis_index("x")

    def part_for(step):
        at = lax.rem(here + step, x_n) * line_rows
        gate = lax.dynamic_slice_in_dim(grad_gate[0], at, line_rows)
        up = lax.dynamic_slice_in_dim(grad_up[0], at, line_rows)
        return lax.dot_general(
            gate, w_gate[0], unit_contract, preferred_element_type=jnp.float32
        ) + lax.dot_general(up, w_up[0], unit_contract, preferred_element_type=jnp.float32)

    arriving = []
    for step in (2, 1, 3):
        piece = part_for(step).astype(jnp.bfloat16)
        arriving.append(along(piece, "x", step).astype(jnp.float32))

    code = (expert_ids * CAP + slot_ids).astype(jnp.bfloat16)
    tagged = jnp.concatenate([tokens, jnp.pad(code, ((0, 0), (0, LANES - 2)))], axis=1)
    line = copy_for_each(tagged, RING).reshape(line_tokens, width + LANES)
    line_values = line[:, :width]
    codes = line[:, width : width + 2].astype(jnp.int32)
    token = jnp.arange(line_tokens, dtype=jnp.int32)
    block = token // TOK
    base = (((block % zl_n) * zh_n + block // zl_n) * core_n + core) * CAP

    def rows_of(expert):
        slot = codes - expert * CAP
        return jnp.where((slot >= 0) & (slot < CAP), base[:, None] + slot, -1)

    row = jnp.arange(line_rows, dtype=jnp.int32)

    def choice(expert):
        at = rows_of(expert)
        return ((at[:, 0][:, None] == row[None]) | (at[:, 1][:, None] == row[None])).astype(
            jnp.bfloat16
        )

    to_mine = choice(mine)
    to_partner = choice(partner)
    first = (((0,), (0,)), ((), ()))

    def rows_from(chosen):
        return lax.dot_general(
            chosen, line_values, first, preferred_element_type=jnp.float32
        ).astype(jnp.bfloat16)

    for_partner = rows_from(to_partner)
    from_partner = swap_cores(for_partner)
    own_rows = rows_from(to_mine) + from_partner
    steps = (0, 1, 3, 2)
    pieces = [own_rows]
    pieces += [along(own_rows, "x", step) for step in steps[1:]]

    line_sum = (part_for(0) + arriving[0] + arriving[1] + arriving[2]).astype(jnp.bfloat16)
    other_sum = swap_cores(line_sum)
    by_token = jnp.dot(to_mine, line_sum, preferred_element_type=jnp.float32) + jnp.dot(
        to_partner, other_sum, preferred_element_type=jnp.float32
    )
    by_token = by_token.astype(jnp.bfloat16).reshape(ring_n, TOK, width)
    normed_grad = exchange(by_token, RING).astype(jnp.float32).sum(axis=0)

    scaled = normed_grad * norm_gain

    values = tokens.astype(jnp.float32)
    totals = [jnp.sum(jnp.square(piece.astype(jnp.float32)), axis=1) for piece in pieces]
    totals += [jnp.sum(values * values, axis=1), jnp.sum(scaled * values, axis=1)]
    rows_n = x_n * line_rows
    count = rows_n + 2 * TOK
    totals = jnp.pad(jnp.concatenate(totals), (0, -count % LANES))
    totals = feature_total(totals)
    rms = lax.rsqrt(totals[: rows_n + TOK] / D + 1e-05)[:, None]
    row_rms, inverse_rms = rms[:rows_n], rms[rows_n:]
    dotted = inverse_rms * totals[rows_n + TOK : count, None] / D
    grad_tokens = (inverse_rms * (scaled - values * inverse_rms * dotted)).astype(jnp.bfloat16)

    raw = jnp.concatenate(pieces).astype(jnp.float32)
    gathered = (raw * row_rms * norm_gain).astype(jnp.bfloat16)

    def in_order(cotangent):
        return jnp.concatenate(
            [
                lax.dynamic_slice_in_dim(
                    cotangent, lax.rem(here - step + x_n, x_n) * line_rows, line_rows
                )
                for step in steps
            ]
        )

    new_gate = lax.dot_general(
        gathered, in_order(grad_gate[0]), first, preferred_element_type=jnp.float32
    )
    new_up = lax.dot_general(
        gathered, in_order(grad_up[0]), first, preferred_element_type=jnp.float32
    )

    return (new_gate.astype(jnp.bfloat16)[None], new_up.astype(jnp.bfloat16)[None], grad_tokens)


def solution(mesh):
    physical = Mesh(mesh.devices.reshape(2, 2, 4, 4, 8), ("zh", "core", "rep", "x", "zl"))
    expert, hid = ("zh", "core"), ("x", "zl")
    placed = (
        P(expert + hid, "rep"),
        P("rep"),
        P(expert + hid, None),
        P(expert + hid, None),
        P(expert, "rep", hid),
        P(expert, "rep", hid),
        P(expert, None, hid),
        P(expert, None, hid),
    )

    return jax.shard_map(
        on_device,
        mesh=physical,
        in_specs=placed,
        out_specs=(P(expert, "rep", hid), P(expert, "rep", hid), P(expert + hid, "rep")),
        check_vma=False,
    )
```

```python
import jax
import jax.numpy as jnp
from jax import lax
from jax.sharding import Mesh
from jax.sharding import PartitionSpec as P


D = 6144
CAP = 5
TOK = 8
RING = ("zh", "zl")
LANES = 128


def exchange(x, axis):
    return lax.all_to_all(x, axis, 0, 0, tiled=True)


def copy_for_each(x, axis):
    size = lax.axis_size(axis)
    return exchange(jnp.broadcast_to(x[None], (size, *x.shape)), axis)


def feature_total(partial_value):
    return copy_for_each(partial_value[None], "rep").sum(axis=(0, 1))


def along_x(x, step):
    size = lax.axis_size("x")
    return lax.ppermute(x, "x", [(i, (i + step) % size) for i in range(size)])


def swap_cores(x):
    return lax.ppermute(x, "core", [(0, 1), (1, 0)])


def on_device(tokens, norm_gain, expert_ids, slot_ids, w_gate, w_up, grad_gate, grad_up):
    zh_n, core_n, x_n, zl_n = (lax.axis_size(a) for a in ("zh", "core", "x", "zl"))
    ring_n = zh_n * zl_n
    line_tokens = ring_n * TOK
    line_rows = zl_n * zh_n * core_n * CAP
    width = tokens.shape[1]
    core = lax.axis_index("core")
    mine = lax.axis_index("zh") * core_n + core
    partner = lax.axis_index("zh") * core_n + (1 - core)

    unit_contract = (((1,), (1,)), ((), ()))
    here = lax.axis_index("x")

    def part_for(step):
        at = lax.rem(here + step, x_n) * line_rows
        gate = lax.dynamic_slice_in_dim(grad_gate[0], at, line_rows)
        up = lax.dynamic_slice_in_dim(grad_up[0], at, line_rows)
        return lax.dot_general(
            gate, w_gate[0], unit_contract, preferred_element_type=jnp.float32
        ) + lax.dot_general(up, w_up[0], unit_contract, preferred_element_type=jnp.float32)

    arriving = []
    for step in (2, 1, 3):
        piece = part_for(step).astype(jnp.bfloat16)
        arriving.append(along_x(piece, step).astype(jnp.float32))

    values = tokens.astype(jnp.float32)
    square_sums = feature_total(jnp.sum(values * values, axis=1))
    inverse_rms = lax.rsqrt(square_sums / D + 1e-05)[:, None]
    scaled_in = values * inverse_rms
    normed = (scaled_in * norm_gain).astype(jnp.bfloat16)
    code = (expert_ids * CAP + slot_ids).astype(jnp.bfloat16)
    tagged = jnp.concatenate([normed, jnp.pad(code, ((0, 0), (0, LANES - 2)))], axis=1)

    line = copy_for_each(tagged, RING).reshape(line_tokens, width + LANES)
    line_normed = line[:, :width]
    codes = line[:, width : width + 2].astype(jnp.int32)
    token = jnp.arange(line_tokens, dtype=jnp.int32)
    block = token // TOK
    base = (((block % zl_n) * zh_n + block // zl_n) * core_n + core) * CAP

    def rows_of(expert):
        slot = codes - expert * CAP
        return jnp.where((slot >= 0) & (slot < CAP), base[:, None] + slot, -1)

    row = jnp.arange(line_rows, dtype=jnp.int32)

    def choice(expert):
        at = rows_of(expert)
        return ((at[:, 0][:, None] == row[None]) | (at[:, 1][:, None] == row[None])).astype(
            jnp.bfloat16
        )

    to_mine = choice(mine)
    to_partner = choice(partner)
    first = (((0,), (0,)), ((), ()))

    def rows_from(chosen):
        return lax.dot_general(
            chosen, line_normed, first, preferred_element_type=jnp.float32
        ).astype(jnp.bfloat16)

    for_partner = rows_from(to_partner)
    from_partner = swap_cores(for_partner)
    own_rows = rows_from(to_mine) + from_partner
    steps = (0, 1, 3, 2)
    gathered = jnp.concatenate([own_rows] + [along_x(own_rows, step) for step in steps[1:]])

    def in_order(cotangent):
        return jnp.concatenate(
            [
                lax.dynamic_slice_in_dim(
                    cotangent, lax.rem(here - step + x_n, x_n) * line_rows, line_rows
                )
                for step in steps
            ]
        )

    new_gate = lax.dot_general(
        gathered, in_order(grad_gate[0]), first, preferred_element_type=jnp.float32
    )
    new_up = lax.dot_general(
        gathered, in_order(grad_up[0]), first, preferred_element_type=jnp.float32
    )

    line_sum = (part_for(0) + arriving[0] + arriving[1] + arriving[2]).astype(jnp.bfloat16)
    other_sum = swap_cores(line_sum)
    by_token = jnp.dot(to_mine, line_sum, preferred_element_type=jnp.float32) + jnp.dot(
        to_partner, other_sum, preferred_element_type=jnp.float32
    )
    by_token = by_token.astype(jnp.bfloat16).reshape(ring_n, TOK, width)
    normed_grad = exchange(by_token, RING).astype(jnp.float32).sum(axis=0)

    scaled = normed_grad * norm_gain
    partial_dots = jnp.sum(scaled * scaled_in, axis=1)
    dotted = feature_total(partial_dots) / D
    grad_tokens = (inverse_rms * (scaled - scaled_in * dotted[:, None])).astype(jnp.bfloat16)
    return (new_gate.astype(jnp.bfloat16)[None], new_up.astype(jnp.bfloat16)[None], grad_tokens)


def solution(mesh):
    physical = Mesh(mesh.devices.reshape(2, 2, 4, 4, 8), ("zh", "core", "rep", "x", "zl"))
    expert, hid = ("zh", "core"), ("x", "zl")
    placed = (
        P(expert + hid, "rep"),
        P("rep"),
        P(expert + hid, None),
        P(expert + hid, None),
        P(expert, "rep", hid),
        P(expert, "rep", hid),
        P(expert, None, hid),
        P(expert, None, hid),
    )

    return jax.shard_map(
        on_device,
        mesh=physical,
        in_specs=placed,
        out_specs=(P(expert, "rep", hid), P(expert, "rep", hid), P(expert + hid, "rep")),
        check_vma=False,
    )
```

```python
import jax
import jax.numpy as jnp
from jax import lax
from jax.sharding import Mesh
from jax.sharding import PartitionSpec as P


D = 6144
CAP = 5
TOK = 8
RING = ("zh", "zl")
LANES = 128


def exchange(x, axis):
    return lax.all_to_all(x, axis, 0, 0, tiled=True)


def copy_for_each(x, axis):
    size = lax.axis_size(axis)
    return exchange(jnp.broadcast_to(x[None], (size, *x.shape)), axis)


def feature_total(partial_value):
    return copy_for_each(partial_value[None], "rep").sum(axis=(0, 1))


def along_x(x, step):
    size = lax.axis_size("x")
    return lax.ppermute(x, "x", [(i, (i + step) % size) for i in range(size)])


def swap_cores(x):
    return lax.ppermute(x, "core", [(0, 1), (1, 0)])


def on_device(tokens, norm_gain, expert_ids, slot_ids, w_gate, w_up, grad_gate, grad_up):
    zh_n, core_n, x_n, zl_n = (lax.axis_size(a) for a in ("zh", "core", "x", "zl"))
    ring_n = zh_n * zl_n
    line_tokens = ring_n * TOK
    line_rows = zl_n * zh_n * core_n * CAP
    width = tokens.shape[1]
    core = lax.axis_index("core")
    mine = lax.axis_index("zh") * core_n + core
    partner = lax.axis_index("zh") * core_n + (1 - core)

    unit_contract = (((1,), (1,)), ((), ()))
    here = lax.axis_index("x")

    def part_for(step):
        at = lax.rem(here + step, x_n) * line_rows
        gate = lax.dynamic_slice_in_dim(grad_gate[0], at, line_rows)
        up = lax.dynamic_slice_in_dim(grad_up[0], at, line_rows)
        return lax.dot_general(
            gate, w_gate[0], unit_contract, preferred_element_type=jnp.float32
        ) + lax.dot_general(up, w_up[0], unit_contract, preferred_element_type=jnp.float32)

    arriving = []
    for step in (2, 1, 3):
        piece = part_for(step).astype(jnp.bfloat16)
        arriving.append(along_x(piece, step).astype(jnp.float32))

    values = tokens.astype(jnp.float32)
    square_sums = feature_total(jnp.sum(values * values, axis=1))
    inverse_rms = lax.rsqrt(square_sums / D + 1e-05)[:, None]
    scaled_in = values * inverse_rms
    normed = (scaled_in * norm_gain).astype(jnp.bfloat16)
    code = (expert_ids * CAP + slot_ids).astype(jnp.bfloat16)
    tagged = jnp.concatenate([normed, jnp.pad(code, ((0, 0), (0, LANES - 2)))], axis=1)

    line = copy_for_each(tagged, RING).reshape(line_tokens, width + LANES)
    line_normed = line[:, :width]
    codes = line[:, width : width + 2].astype(jnp.int32)
    token = jnp.arange(line_tokens, dtype=jnp.int32)
    block = token // TOK
    base = (((block % zl_n) * zh_n + block // zl_n) * core_n + core) * CAP

    def rows_of(expert):
        slot = codes - expert * CAP
        return jnp.where((slot >= 0) & (slot < CAP), base[:, None] + slot, -1)

    row = jnp.arange(line_rows, dtype=jnp.int32)

    def choice(expert):
        at = rows_of(expert)
        return ((at[:, 0][:, None] == row[None]) | (at[:, 1][:, None] == row[None])).astype(
            jnp.bfloat16
        )

    to_mine = choice(mine)
    to_partner = choice(partner)
    first = (((0,), (0,)), ((), ()))

    def rows_from(chosen):
        return lax.dot_general(
            chosen, line_normed, first, preferred_element_type=jnp.float32
        ).astype(jnp.bfloat16)

    for_partner = rows_from(to_partner)
    from_partner = swap_cores(for_partner)
    own_rows = rows_from(to_mine) + from_partner
    steps = (0, 1, 3, 2)
    gathered = jnp.concatenate([own_rows] + [along_x(own_rows, step) for step in steps[1:]])

    def in_order(cotangent):
        return jnp.concatenate(
            [
                lax.dynamic_slice_in_dim(
                    cotangent, lax.rem(here - step + x_n, x_n) * line_rows, line_rows
                )
                for step in steps
            ]
        )

    gate_rows, up_rows = lax.optimization_barrier(
        (in_order(grad_gate[0]), in_order(grad_up[0]))
    )
    gathered = lax.optimization_barrier(gathered)
    new_gate = lax.dot_general(
        gathered, gate_rows, first, preferred_element_type=jnp.float32
    )
    new_up = lax.dot_general(
        gathered, up_rows, first, preferred_element_type=jnp.float32
    )

    line_sum = (part_for(0) + arriving[0] + arriving[1] + arriving[2]).astype(jnp.bfloat16)
    other_sum = swap_cores(line_sum)
    by_token = jnp.dot(to_mine, line_sum, preferred_element_type=jnp.float32) + jnp.dot(
        to_partner, other_sum, preferred_element_type=jnp.float32
    )
    by_token = by_token.astype(jnp.bfloat16).reshape(ring_n, TOK, width)
    normed_grad = exchange(by_token, RING).astype(jnp.float32).sum(axis=0)

    scaled = normed_grad * norm_gain
    partial_dots = jnp.sum(scaled * scaled_in, axis=1)
    dotted = feature_total(partial_dots) / D
    grad_tokens = (inverse_rms * (scaled - scaled_in * dotted[:, None])).astype(jnp.bfloat16)
    return (new_gate.astype(jnp.bfloat16)[None], new_up.astype(jnp.bfloat16)[None], grad_tokens)


def solution(mesh):
    physical = Mesh(mesh.devices.reshape(2, 2, 4, 4, 8), ("zh", "core", "rep", "x", "zl"))
    expert, hid = ("zh", "core"), ("x", "zl")
    placed = (
        P(expert + hid, "rep"),
        P("rep"),
        P(expert + hid, None),
        P(expert + hid, None),
        P(expert, "rep", hid),
        P(expert, "rep", hid),
        P(expert, None, hid),
        P(expert, None, hid),
    )

    return jax.shard_map(
        on_device,
        mesh=physical,
        in_specs=placed,
        out_specs=(P(expert, "rep", hid), P(expert, "rep", hid), P(expert + hid, "rep")),
        check_vma=False,
    )
```

```python
import jax
import jax.numpy as jnp
from jax import lax
from jax.sharding import Mesh
from jax.sharding import PartitionSpec as P


D = 6144
CAP = 5
TOK = 8
RING = ("zh", "zl")
LANES = 128


def exchange(x, axis):
    return lax.all_to_all(x, axis, 0, 0, tiled=True)


def copy_for_each(x, axis):
    size = lax.axis_size(axis)
    return exchange(jnp.broadcast_to(x[None], (size, *x.shape)), axis)


def feature_total(partial_value):
    return copy_for_each(partial_value[None], "rep").sum(axis=(0, 1))


def along_x(x, step):
    size = lax.axis_size("x")
    return lax.ppermute(x, "x", [(i, (i + step) % size) for i in range(size)])


def swap_cores(x):
    return lax.ppermute(x, "core", [(0, 1), (1, 0)])


def on_device(tokens, norm_gain, expert_ids, slot_ids, w_gate, w_up, grad_gate, grad_up):
    zh_n, core_n, x_n, zl_n = (lax.axis_size(a) for a in ("zh", "core", "x", "zl"))
    ring_n = zh_n * zl_n
    line_tokens = ring_n * TOK
    line_rows = zl_n * zh_n * core_n * CAP
    width = tokens.shape[1]
    core = lax.axis_index("core")
    mine = lax.axis_index("zh") * core_n + core
    partner = lax.axis_index("zh") * core_n + (1 - core)

    unit_contract = (((1,), (1,)), ((), ()))
    here = lax.axis_index("x")

    def part_for(step):
        at = lax.rem(here + step, x_n) * line_rows
        gate = lax.dynamic_slice_in_dim(grad_gate[0], at, line_rows)
        up = lax.dynamic_slice_in_dim(grad_up[0], at, line_rows)
        return lax.dot_general(
            gate, w_gate[0], unit_contract, preferred_element_type=jnp.float32
        ) + lax.dot_general(up, w_up[0], unit_contract, preferred_element_type=jnp.float32)

    arriving = []
    for step in (2, 1, 3):
        piece = part_for(step).astype(jnp.bfloat16)
        arriving.append(along_x(piece, step).astype(jnp.float32))

    values = tokens.astype(jnp.float32)
    square_sums = feature_total(jnp.sum(values * values, axis=1))
    inverse_rms = lax.rsqrt(square_sums / D + 1e-05)[:, None]
    scaled_in = values * inverse_rms
    normed = (scaled_in * norm_gain).astype(jnp.bfloat16)
    code = (expert_ids * CAP + slot_ids).astype(jnp.bfloat16)
    tagged = jnp.concatenate([normed, jnp.pad(code, ((0, 0), (0, LANES - 2)))], axis=1)

    line = copy_for_each(tagged, RING).reshape(line_tokens, width + LANES)
    line_normed = line[:, :width]
    codes = line[:, width : width + 2].astype(jnp.int32)
    token = jnp.arange(line_tokens, dtype=jnp.int32)
    block = token // TOK
    base = (((block % zl_n) * zh_n + block // zl_n) * core_n + core) * CAP

    def rows_of(expert):
        slot = codes - expert * CAP
        return jnp.where((slot >= 0) & (slot < CAP), base[:, None] + slot, -1)

    row = jnp.arange(line_rows, dtype=jnp.int32)

    def choice(expert):
        at = rows_of(expert)
        return ((at[:, 0][:, None] == row[None]) | (at[:, 1][:, None] == row[None])).astype(
            jnp.bfloat16
        )

    to_mine = choice(mine)
    to_partner = choice(partner)
    first = (((0,), (0,)), ((), ()))

    def rows_from(chosen):
        return lax.dot_general(
            chosen, line_normed, first, preferred_element_type=jnp.float32
        ).astype(jnp.bfloat16)

    for_partner = rows_from(to_partner)
    from_partner = swap_cores(for_partner)
    own_rows = rows_from(to_mine) + from_partner
    steps = (0, 1, 3, 2)
    pieces = [own_rows]
    for step in steps[1:]:
        pieces.append(along_x(own_rows, step))
    gathered = jnp.concatenate(pieces)

    def in_order(cotangent):
        return jnp.concatenate(
            [
                lax.dynamic_slice_in_dim(
                    cotangent, lax.rem(here - step + x_n, x_n) * line_rows, line_rows
                )
                for step in steps
            ]
        )

    gate_rows, up_rows = lax.optimization_barrier(
        (in_order(grad_gate[0]), in_order(grad_up[0]))
    )
    gathered = lax.optimization_barrier(gathered)
    new_gate = lax.dot_general(
        gathered, gate_rows, first, preferred_element_type=jnp.float32
    )
    new_up = lax.dot_general(
        gathered, up_rows, first, preferred_element_type=jnp.float32
    )

    line_sum = (part_for(0) + arriving[0] + arriving[1] + arriving[2]).astype(jnp.bfloat16)
    other_sum = swap_cores(line_sum)
    by_token = jnp.dot(to_mine, line_sum, preferred_element_type=jnp.float32) + jnp.dot(
        to_partner, other_sum, preferred_element_type=jnp.float32
    )
    by_token = by_token.astype(jnp.bfloat16).reshape(ring_n, TOK, width)
    normed_grad = exchange(by_token, RING).astype(jnp.float32).sum(axis=0)

    scaled = normed_grad * norm_gain
    partial_dots = jnp.sum(scaled * scaled_in, axis=1)
    dotted = feature_total(partial_dots) / D
    grad_tokens = (inverse_rms * (scaled - scaled_in * dotted[:, None])).astype(jnp.bfloat16)
    return (new_gate.astype(jnp.bfloat16)[None], new_up.astype(jnp.bfloat16)[None], grad_tokens)


def solution(mesh):
    physical = Mesh(mesh.devices.reshape(2, 2, 4, 4, 8), ("zh", "core", "rep", "x", "zl"))
    expert, hid = ("zh", "core"), ("x", "zl")
    placed = (
        P(expert + hid, "rep"),
        P("rep"),
        P(expert + hid, None),
        P(expert + hid, None),
        P(expert, "rep", hid),
        P(expert, "rep", hid),
        P(expert, None, hid),
        P(expert, None, hid),
    )

    return jax.shard_map(
        on_device,
        mesh=physical,
        in_specs=placed,
        out_specs=(P(expert, "rep", hid), P(expert, "rep", hid), P(expert + hid, "rep")),
        check_vma=False,
    )
```
